128 devices in a mesh: dp: 32 (over x, y, core), tensor: 4 (over z).
Axes of the slice: x: 4, y: 4, z: 4, core: 2. Of those that a mesh axis runs over, the one named last changes fastest.
Arguments:
- activations: bfloat16 [32, 1536, 2048], P('dp', 'tensor'), may hold values from -6 to 6
- upstream_grad: bfloat16 [32, 1536, 4096], P('dp', None, 'tensor'), may hold values from -0.15625 to 0.15625
- feedback: bfloat16 [32, 2048, 4096], P('dp', None, 'tensor'), may hold values from -3 to 3
- selected: int32 [32, 4, 2], P('dp', 'tensor'), may hold values from -1 to 255, as said below
- cycle_values: bfloat16 [8, 4, 64, 64, 128], P(None, 'tensor'), may hold values from -6 to 6
- cycle_blocks: int32 [8, 4, 64], P(None, 'tensor'), may hold values from -1 to 255, as said below
- cycle_position: int32 [1], replicated, may hold values from 0 to 7
Outputs:
- update_dir: bfloat16 [2048, 4096], P(None, 'tensor')
- new_feedback: bfloat16 [32, 2048, 4096], P('dp', None, 'tensor')
- newest_values: bfloat16 [4, 64, 64, 128], P('tensor')
The draws below stay inside these ranges and needn't reach their ends.
Inputs may be any that keep to these rules, and one draw needn't show every extreme that they name: `selected`: for each replica and tensor shard, the 2 entries hold 1 to 2 distinct block numbers first, then -1; in every tensor shard some replica lists 2 blocks. `cycle_blocks`: within each slot and tensor shard, entries r * 2 to r * 2 + 1 hold 1 to 2 distinct block numbers first, then -1; in every slot and shard some group of 2 entries is full.
All inputs are finite; a program needn't handle non-finite values.
Results may differ from the reference program's by a relative error of at most 0.0023.
Values may be sent and summed in bfloat16 or wider, within the bound.
No kernel may reach another device: no remote copies, remote signals or barrier semaphores. Data moves between devices by JAX's collectives and lax.ppermute only.
A program may use at most 192 MiB of HBM per device.

```python
import jax
import jax.numpy as jnp
from jax import lax

D = 2048
Q = 4096
BH = 64
BW = 128
K = 2
SLOTS = 8
ROWS = 1536
QS = 1024
NBLK = 256
ENTRIES = 64
N_DP = 32
N_TENSOR = 4


def listed_table(key, outer_count, groups):
    count_key, full_key, order_key = jax.random.split(key, 3)
    counts = jax.random.randint(count_key, (outer_count, groups), 1, K + 1)
    fullest = jax.random.randint(full_key, (outer_count,), 0, groups)
    counts = jnp.where(jnp.arange(groups)[None, :] == fullest[:, None], K, counts)
    order_keys = jax.random.split(order_key, outer_count * groups)
    chosen = jax.vmap(lambda single: jax.random.permutation(single, NBLK)[:K])(order_keys)
    chosen = chosen.reshape(outer_count, groups, K).astype(jnp.int32)
    slot_rank = jnp.arange(K)[None, None, :]
    return jnp.where(slot_rank < counts[:, :, None], chosen, -1).astype(jnp.int32)


def draw_selected(key, part):
    listed = listed_table(jax.random.fold_in(key, 11), N_TENSOR, N_DP)
    return jnp.transpose(listed, (1, 0, 2))


def draw_cycle_blocks(key, part):
    listed = listed_table(jax.random.fold_in(key, 23), SLOTS * N_TENSOR, N_DP)
    return listed.reshape(SLOTS, N_TENSOR, N_DP * K)


def steps_of(key, dims, pieces, low, high):
    def one(dim, blocks):
        steps = jax.random.uniform(jax.random.fold_in(jax.random.fold_in(key, 6), dim), (blocks,), jnp.float32, low / len(pieces), high / len(pieces))
        return jnp.repeat(jnp.exp(steps), dims[dim] // blocks).reshape((-1,) + (1,) * (len(dims) - dim - 1))

    gain = one(*pieces[0])
    for cut in pieces[1:]:
        gain = gain * one(*cut)
    return gain


def centred(own_key, shape, width, limit, cuts=(), dtype=jnp.bfloat16):
    entries = width * jax.random.normal(own_key, shape, jnp.float32)
    if cuts:
        entries = entries * steps_of(own_key, shape, cuts, -0.22, 0.18)
    return jnp.clip(entries, -limit, limit).astype(dtype)


def setup_inputs(seed: int = 0) -> dict:
    splits = jax.random.split(jax.random.key(seed), 8)
    activations = centred(splits[0], (N_DP, ROWS, D), 1.0, 6.0, ((0, 32), (1, 4)))
    upstream_grad = centred(splits[1], (N_DP, ROWS, Q), 0.025, 0.15625, ((0, 32), (2, 4)))
    feedback = centred(splits[2], (N_DP, D, Q), 0.5, 3.0, ((0, 32), (2, 4)))
    selected = draw_selected(jax.random.fold_in(splits[7], 71), 0)
    cycle_values = centred(splits[4], (SLOTS, N_TENSOR, ENTRIES, BH, BW), 1.0, 6.0, ((1, 4),))
    cycle_blocks = draw_cycle_blocks(jax.random.fold_in(splits[7], 71), 0)
    cycle_position = jax.random.randint(splits[6], (1,), 0, SLOTS).astype(jnp.int32)
    return dict(activations=activations, upstream_grad=upstream_grad, feedback=feedback, selected=selected, cycle_values=cycle_values, cycle_blocks=cycle_blocks, cycle_position=cycle_position)


decay_first = 0.9
decay_second = 0.999
epsilon = 0.001

def to_blocks(matrix):
    row_blocks = matrix.shape[0] // BH
    col_blocks = matrix.shape[1] // BW
    return matrix.reshape(row_blocks, BH, col_blocks, BW).transpose(0, 2, 1, 3).reshape(row_blocks * col_blocks, BH, BW)

def from_blocks(blocks, height, breadth):
    return blocks.reshape(height // BH, breadth // BW, BH, BW).transpose(0, 2, 1, 3).reshape(height, breadth)

def one_replica(inputs):
    token_rows, upstream, feedback_one, listed = inputs
    gradient = jnp.dot(token_rows.T, upstream, preferred_element_type=jnp.float32)
    accumulated = gradient + feedback_one.astype(jnp.float32)
    shards = accumulated.reshape(D, N_TENSOR, QS).transpose(1, 0, 2)
    blocks = jax.vmap(to_blocks)(shards)
    is_live = listed >= 0
    safe_index = jnp.where(is_live, listed, 0)
    outgoing = jax.vmap(lambda grid, index_row: grid[index_row])(blocks, safe_index)
    outgoing = (outgoing * is_live[:, :, None, None]).astype(jnp.bfloat16)
    cleared = jnp.any(jnp.arange(NBLK)[None, :, None] == listed[:, None, :], axis=2)
    remaining = jnp.where(cleared[:, :, None, None], 0.0, blocks)
    merged = jax.vmap(lambda grid: from_blocks(grid, D, QS))(remaining)
    return (merged.transpose(1, 0, 2).reshape(D, Q).astype(jnp.bfloat16), outgoing)

def densify(values, listed):
    is_live = listed >= 0
    safe_index = jnp.where(is_live, listed, 0)
    terms = values.astype(jnp.float32) * is_live[:, None, None]
    return jnp.zeros((NBLK, BH, BW), jnp.float32).at[safe_index].add(terms)

def reference(activations, upstream_grad, feedback, selected, cycle_values, cycle_blocks, cycle_position):
    new_feedback, outgoing = lax.map(one_replica, (activations, upstream_grad, feedback, selected))
    newest_values = outgoing.transpose(1, 0, 2, 3, 4).reshape(N_TENSOR, ENTRIES, BH, BW)
    newest_blocks = selected.transpose(1, 0, 2).reshape(N_TENSOR, ENTRIES)
    position = cycle_position[0]
    first_moment = jnp.zeros((N_TENSOR, NBLK, BH, BW), jnp.float32)
    second_moment = jnp.zeros((N_TENSOR, NBLK, BH, BW), jnp.float32)
    for slot_number in range(SLOTS):
        newest = position == slot_number
        values = jnp.where(newest, newest_values, cycle_values[slot_number])
        listed = jnp.where(newest, newest_blocks, cycle_blocks[slot_number])
        densified = jax.vmap(densify)(values, listed)
        slot_age = jnp.mod(position - slot_number, SLOTS).astype(jnp.float32)
        weight_first = (1.0 - decay_first) * jnp.power(decay_first, slot_age)
        weight_second = (1.0 - decay_second) * jnp.power(decay_second, slot_age)
        first_moment = first_moment + weight_first * densified
        second_moment = second_moment + weight_second * (densified * densified)
    update = first_moment / (jnp.sqrt(second_moment) + epsilon)
    merged = jax.vmap(lambda grid: from_blocks(grid, D, QS))(update)
    update_dir = merged.transpose(1, 0, 2).reshape(D, Q).astype(jnp.bfloat16)
    return (update_dir, new_feedback, newest_values)
```

```python
import functools

import jax
import jax.numpy as jnp
from jax import lax
from jax.experimental import pallas as pl
from jax.experimental.pallas import tpu as pltpu
from jax.sharding import PartitionSpec as P

D = 2048
QS = 1024
BH = 64
BW = 128
K = 2
SLOTS = 8
NBLK = 256
ENTRIES = 64
NX = 4
NY = 4
NC = 2
NZ = 4
N_DP = 32
TOK = 384
ROWS = 1536
NOTE = 16
QUARTER = D // 4
HALF = D // 2
TOTAL = SLOTS * ENTRIES

decay_first = 0.9
decay_second = 0.999
epsilon = 0.001

CONTRACT = (((0,), (0,)), ((), ()))
SMEM = pltpu.SMEM
VMEM = pltpu.VMEM
F32 = jnp.float32
BF16 = jnp.bfloat16


def whole(space):
    return pl.BlockSpec(memory_space=space)


def params(mb):
    return pltpu.CompilerParams(vmem_limit_bytes=mb << 20)


def cost(flops, moved):
    return pl.CostEstimate(flops=1, bytes_accessed=1, transcendentals=0)


def shift(x, axis, size, step):
    return lax.ppermute(x, axis, [(i, (i + step) % size) for i in range(size)])


FLIPS = (0, 1, 3, 2)


def pass_on(x, flip):
    return lax.ppermute(x, "tensor", [(i, i ^ flip) for i in range(NZ)])


def swap(x, flip):
    return jnp.concatenate([x, pass_on(x, flip)])


def dp_index(x, y, c):
    return (x * NY + y) * NC + c


def dp_exchange(value, partner):
    pairs = []
    for x in range(NX):
        for y in range(NY):
            for c in range(NC):
                pairs.append((dp_index(x, y, c), dp_index(*partner(x, y, c))))
    return jnp.concatenate([value, lax.ppermute(value, "dp", pairs)])


def up_rows(up, offset=0, flip=0):
    me = lax.axis_index("tensor").astype(jnp.int32)
    owner = lax.bitwise_xor(lax.rem(me + offset, NZ), flip)
    return up.at[pl.ds(pl.multiple_of(owner * TOK, TOK), TOK), :]


def reply_kernel(asked, tokens, *outs):
    low = lax.broadcasted_iota(jnp.int32, (TOK, BW), 1) < BH
    for i, out in enumerate(outs):
        halves = []
        for k in range(K):
            row = lax.shift_right_logical(jnp.maximum(asked[i * K + k], 0), 3)
            start = pl.multiple_of(lax.shift_right_logical(row, 1) * BW, BW)
            pair = tokens[:, pl.ds(start, BW)].astype(F32)
            turned = pltpu.roll(pair, BH, 1)
            halves.append(jnp.where(lax.bitwise_and(row, 1) == k, pair, turned))
        out[...] = jnp.where(low, halves[0], halves[1]).astype(BF16)


def reply(asked, tokens):
    return pl.pallas_call(
        reply_kernel,
        out_shape=[jax.ShapeDtypeStruct((TOK, K * BH), BF16)] * NZ,
        in_specs=[whole(SMEM), whole(VMEM)],
        out_specs=[whole(VMEM)] * NZ,
        compiler_params=params(4),
        cost_estimate=cost(0, 1 << 20),
        name="reply",
    )(asked, tokens)


def pick_kernel(chosen, up, fb, own, c1, c2, c3, out, block, sem):
    def fetch(k):
        number = jnp.maximum(chosen[k], 0)
        row = pl.multiple_of(lax.shift_right_logical(number, 3) * BH, BH)
        col = pl.multiple_of(lax.bitwise_and(number, 7) * BW, BW)
        return pltpu.make_async_copy(
            fb.at[pl.ds(row, BH), pl.ds(col, BW)], block.at[k], sem.at[k]
        )

    for k in range(K):
        fetch(k).start()
    lane = lax.broadcasted_iota(jnp.int32, (NOTE, BW), 1)
    out[K * BH :, :] = jnp.where(lane == 0, chosen[0], chosen[1]).astype(F32).astype(BF16)
    for k in range(K):
        col = pl.multiple_of(lax.bitwise_and(jnp.maximum(chosen[k], 0), 7) * BW, BW)
        total = jnp.zeros((K * BH, BW), F32)
        for flip, ref in zip(FLIPS, (own, c1, c2, c3)):
            total += lax.dot_general(
                ref[...],
                up_rows(up, flip=flip)[:, pl.ds(col, BW)],
                CONTRACT,
                preferred_element_type=F32,
            )
        fetch(k).wait()
        live = jnp.where(chosen[k] >= 0, 1.0, 0.0)
        value = total[k * BH : (k + 1) * BH] + block[k].astype(F32)
        out[k * BH : (k + 1) * BH, :] = (value * live).astype(BF16)


def pick(chosen, up, fb, parts):
    return pl.pallas_call(
        pick_kernel,
        out_shape=jax.ShapeDtypeStruct((K * BH + NOTE, BW), BF16),
        in_specs=[whole(SMEM), whole(VMEM), whole(pl.ANY)] + [whole(VMEM)] * NZ,
        out_specs=whole(VMEM),
        scratch_shapes=[VMEM((K, BH, BW), BF16), pltpu.SemaphoreType.DMA((K,))],
        compiler_params=params(4),
        cost_estimate=cost(2 * K * 128 * ROWS * BW, 2 << 20),
        name="pick",
    )(chosen, up, fb, *parts)


def old_moments(start, nxt, w1, w2, vals):
    def entry(i):
        slot = lax.shift_right_logical(i, 6)
        following = nxt[i]
        last = lax.shift_right_logical(following, 6) != slot
        value = vals[jnp.minimum(i, TOTAL - 1)].astype(F32)
        return slot, following, value, w1[slot], jnp.where(last, w2[slot], 0.0)

    def more(carry):
        return carry[0] < TOTAL

    def body(carry):
        i, before, m1, m2, acc = carry
        slot, following, value, one, two = entry(i)
        acc = value + jnp.where(slot == before, 1.0, 0.0) * acc
        return following, slot, m1 + one * value, m2 + two * acc * acc, acc

    slot, following, value, one, two = entry(start)
    carry = (following, slot, one * value, two * value * value, value)
    _, _, m1, m2, _ = lax.while_loop(more, body, carry)
    return m1, m2


def direction(m1, m2):
    return (m1 / (jnp.sqrt(m2) + epsilon)).astype(BF16)


WSTEP = 4
WPARTS = 2


def window_kernel(base, head, nxt, w1, w2, vals, *refs):
    out = refs[-1]
    first = (base + pl.program_id(0)) * WSTEP

    def row(q, _):
        place = pl.ds(pl.multiple_of(q * BH, BH), BH)
        for col in range(QS // BW):
            m1, m2 = old_moments(head[(first + q) * 8 + col], nxt, w1, w2, vals)
            out[place, col * BW : (col + 1) * BW] = direction(m1, m2)
        return 0

    lax.fori_loop(0, WSTEP, row, 0)


def window(part, head, nxt, w1, w2, vals, earlier):
    steps = D // BH // WSTEP // WPARTS
    base = part * steps
    extra = [] if earlier is None else [earlier]
    return pl.pallas_call(
        functools.partial(window_kernel, base),
        out_shape=jax.ShapeDtypeStruct((D, QS), BF16),
        grid=(steps,),
        in_specs=[whole(SMEM)] * 4 + [whole(VMEM)] + [whole(pl.ANY)] * len(extra),
        out_specs=pl.BlockSpec((WSTEP * BH, QS), lambda i: (base + i, 0)),
        input_output_aliases={5: 0} if extra else {},
        compiler_params=params(4),
        cost_estimate=cost(1e9, 10 << 20),
        name="window",
    )(head, nxt, w1, w2, vals, *extra)


def newest_kernel(
    head, old_nxt, w1, w2, got, vals, update, out, values,
    staged, listed, ids, nxt, first, seen, in_sem, out_sem,
):
    dp = lax.axis_index("dp").astype(jnp.int32)

    def order(r, _):
        place = place_of(lax.bitwise_xor(r, dp))
        for k in range(K):
            values[r * K + k] = got[place, k * BH : (k + 1) * BH]
        note = got[place, K * BH : K * BH + NOTE, :].astype(F32)
        listed[pl.ds(r, 1), :] = note[:1].astype(jnp.int32)
        return 0

    lax.fori_loop(0, N_DP, order, 0)
    fetch = pltpu.make_async_copy(listed, ids, in_sem)
    fetch.start()

    def clear(b, _):
        seen[b] = -1
        return 0

    lax.fori_loop(0, NBLK, clear, 0, unroll=8)
    fetch.wait()

    def number(e):
        return ids[lax.shift_right_logical(e, 1), lax.bitwise_and(e, 1)]

    def chain(e, _):
        block = number(e)
        nxt[e] = ENTRIES
        first[e] = 0

        @pl.when(block >= 0)
        def _():
            before = seen[block]
            seen[block] = e
            first[e] = jnp.where(before < 0, 1, 0)

            @pl.when(before >= 0)
            def _():
                nxt[before] = e

        return 0

    lax.fori_loop(0, ENTRIES, chain, 0)

    def out_copy(e):
        block = number(e)
        row = pl.multiple_of(lax.shift_right_logical(block, 3) * BH, BH)
        col = pl.multiple_of(lax.bitwise_and(block, 7) * BW, BW)
        return pltpu.make_async_copy(
            staged.at[e], out.at[pl.ds(row, BH), pl.ds(col, BW)], out_sem.at[e]
        )

    def finish(e, _):
        @pl.when(first[e] == 1)
        def _():
            def more(carry):
                return carry[0] < ENTRIES

            def body(carry):
                i, acc = carry
                return nxt[i], acc + values[i].astype(F32)

            m1, m2 = old_moments(head[number(e)], old_nxt, w1, w2, vals)
            _, acc = lax.while_loop(more, body, (nxt[e], values[e].astype(F32)))
            m1 = m1 + (1.0 - decay_first) * acc
            m2 = m2 + (1.0 - decay_second) * (acc * acc)
            staged[e] = direction(m1, m2)
            out_copy(e).start()

        return 0

    lax.fori_loop(0, ENTRIES, finish, 0)

    def drain(e, _):
        @pl.when(first[e] == 1)
        def _():
            out_copy(e).wait()

        return 0

    lax.fori_loop(0, ENTRIES, drain, 0)


def place_of(apart):
    core, y, x = apart & 1, (apart >> 1) & 3, (apart >> 3) & 3
    return core * 16 + (x ^ (x >> 1)) * 4 + (y ^ (y >> 1))


def newest(head, old_nxt, w1, w2, got, vals, update):
    return pl.pallas_call(
        newest_kernel,
        out_shape=(
            jax.ShapeDtypeStruct((D, QS), BF16),
            jax.ShapeDtypeStruct((ENTRIES, BH, BW), BF16),
        ),
        in_specs=[whole(SMEM)] * 4 + [whole(VMEM)] * 2 + [whole(pl.ANY)],
        out_specs=(whole(pl.ANY), whole(VMEM)),
        scratch_shapes=[
            VMEM((ENTRIES, BH, BW), BF16),
            VMEM((N_DP, BW), jnp.int32),
            SMEM((N_DP, BW), jnp.int32),
            SMEM((ENTRIES,), jnp.int32),
            SMEM((ENTRIES,), jnp.int32),
            SMEM((NBLK,), jnp.int32),
            pltpu.SemaphoreType.DMA,
            pltpu.SemaphoreType.DMA((ENTRIES,)),
        ],
        input_output_aliases={6: 0},
        compiler_params=params(4),
        cost_estimate=cost(1e9, 8 << 20),
        name="newest",
    )(head, old_nxt, w1, w2, got, vals, update)


ACC = jax.ShapeDtypeStruct((QUARTER, QS), F32)


def product(tokens, up):
    return lax.dot_general(tokens, up, CONTRACT, preferred_element_type=F32)


def near_total(up, fb, a, pieces, q):
    part = slice(q * QUARTER, (q + 1) * QUARTER)
    total = fb[part, :].astype(F32) + product(a[:, part], up_rows(up)[...])
    for offset, (ref, at) in zip((3, 1), pieces):
        tokens = ref[:, at * QUARTER : (at + 1) * QUARTER]
        total += product(tokens, up_rows(up, offset)[...])
    return total


def middle_kernel(jobs, n_pieces, up, fb, a, *refs):
    pieces, outs = refs[:n_pieces], refs[n_pieces:]
    for (q, right, left), out in zip(jobs, outs):
        near = [(pieces[i], at) for i, at in (right, left)]
        out[...] = near_total(up, fb, a, near, q)


def middle(up, fb, a, pieces, jobs):
    return pl.pallas_call(
        functools.partial(middle_kernel, jobs, len(pieces)),
        out_shape=[ACC] * len(jobs),
        in_specs=[whole(VMEM)] * (3 + len(pieces)),
        out_specs=[whole(VMEM)] * len(jobs),
        compiler_params=params(8),
        cost_estimate=cost(6 * TOK * QUARTER * QS * len(jobs), 4 << 20),
        name="middle",
    )(up, fb, a, *pieces)


NSPLIT = 4


def end_kernel(quarters, chosen, up, *refs):
    n = len(quarters)
    pieces, accs = refs[:n], refs[n : 2 * n]
    out, staged, sem = refs[-3:]
    wide = QS // NSPLIT
    copies = []
    for j, (q, piece, acc) in enumerate(zip(quarters, pieces, accs)):
        for s in range(NSPLIT):
            cols = slice(s * wide, (s + 1) * wide)
            total = acc[:, cols] + product(piece[...], up_rows(up, 2)[:, cols])
            for r in range(QUARTER // BH):
                for c in range(wide // BW):
                    block = (q * QUARTER // BH + r) * 8 + s * (wide // BW) + c
                    cleared = (block == chosen[0]) | (block == chosen[1])
                    part = total[r * BH : (r + 1) * BH, c * BW : (c + 1) * BW]
                    staged[
                        j, r * BH : (r + 1) * BH, s * wide + c * BW : s * wide + (c + 1) * BW
                    ] = jnp.where(cleared, 0.0, part).astype(BF16)
            copies.append(
                pltpu.make_async_copy(
                    staged.at[j, :, cols],
                    out.at[q * QUARTER : (q + 1) * QUARTER, cols],
                    sem.at[j, s],
                )
            )
            copies[-1].start()
    for copy in copies:
        copy.wait()


def end(chosen, up, pieces, accs, quarters, earlier):
    n = len(quarters)
    extra = [] if earlier is None else [earlier]
    return pl.pallas_call(
        functools.partial(end_kernel, quarters),
        out_shape=jax.ShapeDtypeStruct((D, QS), BF16),
        in_specs=[whole(SMEM)] + [whole(VMEM)] * (1 + 2 * n) + [whole(pl.ANY)] * len(extra),
        out_specs=whole(pl.ANY),
        scratch_shapes=[VMEM((n, QUARTER, QS), BF16), pltpu.SemaphoreType.DMA((n, NSPLIT))],
        input_output_aliases={2 + 2 * n: 0} if extra else {},
        compiler_params=params(6),
        cost_estimate=cost(2 * n * TOK * QUARTER * QS, 4 << 20),
        name="end",
    )(chosen, up, *pieces, *accs, *extra)


def after(value, *events):
    return lax.optimization_barrier((value, events))[0]


def local(
    activations, upstream_grad, feedback, selected, cycle_values, cycle_blocks, cycle_position
):
    a = activations[0]
    up = upstream_grad[0]
    fb = feedback[0]
    chosen = selected[0, 0]
    position = cycle_position[0]

    slots = jnp.arange(SLOTS)
    listed = jnp.where(slots[:, None] == position, -1, cycle_blocks.reshape(SLOTS, ENTRIES))
    listed = listed.reshape(-1)
    count = jnp.arange(TOTAL)
    place = jnp.arange(TOTAL + 128)
    row = jnp.concatenate([listed, jnp.full((128,), -2, jnp.int32)])
    later = (row[:, None] == listed[None, :]) & (count[None, :] > place[:, None])
    nxt = jnp.min(jnp.where(later, count[None, :], TOTAL), axis=1)
    here = jnp.arange(NBLK)[:, None] == listed[None, :]
    head = jnp.min(jnp.where(here, count[None, :], TOTAL), axis=1)
    table = jnp.arange(2 * SLOTS)
    age = jnp.mod(position - table, SLOTS).astype(F32)
    inside = table < SLOTS
    w1 = jnp.where(inside, (1.0 - decay_first) * jnp.power(decay_first, age), 0.0)
    w2 = jnp.where(inside, (1.0 - decay_second) * jnp.power(decay_second, age), 0.0)
    vals = cycle_values.reshape(TOTAL, BH, BW)

    first_r, first_l = a[:, :QUARTER], a[:, -QUARTER:]
    right_0 = shift(first_r, "tensor", NZ, 1)
    left_0 = shift(first_l, "tensor", NZ, -1)
    known = swap(chosen, 1)
    asked = swap(known, 3)

    parts = reply(asked, a)
    replies = [pass_on(parts[i], flip) for i, flip in enumerate(FLIPS) if flip]
    rest = after(a, parts[1], right_0, left_0)
    right_1 = shift(rest[:, QUARTER:HALF], "tensor", NZ, 1)
    left_1 = shift(rest[:, HALF:-QUARTER], "tensor", NZ, -1)

    outgoing = pick(after(chosen, right_0, left_0), up, fb, [parts[0], *replies])
    rest = after(a, outgoing)
    right_2 = shift(rest[:, HALF:], "tensor", NZ, 1)
    left_2 = shift(rest[:, :HALF], "tensor", NZ, -1)

    got_1 = dp_exchange(outgoing[None], lambda x, y, c: (x, y ^ 1, c))
    update = window(0, after(head, got_1), nxt, w1, w2, vals, None)
    got_1 = after(got_1, update, right_1, left_1)
    got_2 = dp_exchange(got_1, lambda x, y, c: (x, y ^ 3, c))
    got_3 = dp_exchange(got_2, lambda x, y, c: (x ^ 1, y, c))
    update = window(1, after(head, got_2), nxt, w1, w2, vals, update)
    got_4 = dp_exchange(after(got_3, update), lambda x, y, c: (x ^ 3, y, c))
    got = dp_exchange(after(got_4, right_2, left_2), lambda x, y, c: (x, y, c ^ 1))

    far_0 = shift(after(right_0, got_2), "tensor", NZ, 1)
    far_3 = shift(after(left_0, got_2), "tensor", NZ, -1)
    far_1 = shift(right_1[:, :QUARTER], "tensor", NZ, 1)
    far_2 = shift(left_1[:, -QUARTER:], "tensor", NZ, -1)

    update_dir, newest_values = newest(head, nxt, w1, w2, got, vals, update)

    near = [right_0, right_1, right_2, left_0, left_1, left_2]
    q1, q2 = middle(up, fb, a, near, ((1, (1, 0), (5, 1)), (2, (2, 0), (4, 0))))
    q0, q3 = middle(
        up, fb, after(a, far_0, far_3), near, ((0, (0, 0), (5, 0)), (3, (2, 1), (3, 0)))
    )
    merged = end(chosen, up, [far_0, far_3], [q0, q3], (0, 3), None)
    merged = end(chosen, up, [far_1, far_2], [q1, q2], (1, 2), merged)
    return (update_dir, merged[None], newest_values[None])


def solution(mesh):
    placed = (
        P("dp", "tensor", None),
        P("dp", None, "tensor"),
        P("dp", None, "tensor"),
        P("dp", "tensor", None),
        P(None, "tensor", None, None, None),
        P(None, "tensor", None),
        P(),
    )
    return jax.shard_map(
        local,
        mesh=mesh,
        in_specs=placed,
        out_specs=(P(None, "tensor"), P("dp", None, "tensor"), P("tensor", None, None, None)),
        check_vma=False,
    )
```

```python
import functools

import jax
import jax.numpy as jnp
from jax import lax
from jax.experimental import pallas as pl
from jax.experimental.pallas import tpu as pltpu
from jax.sharding import PartitionSpec as P

D = 2048
QS = 1024
BH = 64
BW = 128
K = 2
SLOTS = 8
NBLK = 256
ENTRIES = 64
NX = 4
NY = 4
NC = 2
NZ = 4
N_DP = 32
TOK = 384
ROWS = 1536
NOTE = 16
QUARTER = D // 4
HALF = D // 2
TOTAL = SLOTS * ENTRIES

decay_first = 0.9
decay_second = 0.999
epsilon = 0.001

CONTRACT = (((0,), (0,)), ((), ()))
SMEM = pltpu.SMEM
VMEM = pltpu.VMEM
F32 = jnp.float32
BF16 = jnp.bfloat16


def whole(space):
    return pl.BlockSpec(memory_space=space)


def params(mb):
    return pltpu.CompilerParams(vmem_limit_bytes=mb << 20)


def cost(flops, moved):
    return pl.CostEstimate(flops=1, bytes_accessed=1, transcendentals=0)


def shift(x, axis, size, step):
    return lax.ppermute(x, axis, [(i, (i + step) % size) for i in range(size)])


FLIPS = (0, 1, 3, 2)


def pass_on(x, flip):
    return lax.ppermute(x, "tensor", [(i, i ^ flip) for i in range(NZ)])


def swap(x, flip):
    return jnp.concatenate([x, pass_on(x, flip)])


def dp_index(x, y, c):
    return (x * NY + y) * NC + c


def dp_exchange(value, partner):
    pairs = []
    for x in range(NX):
        for y in range(NY):
            for c in range(NC):
                pairs.append((dp_index(x, y, c), dp_index(*partner(x, y, c))))
    return jnp.concatenate([value, lax.ppermute(value, "dp", pairs)])


def up_rows(up, offset=0, flip=0):
    me = lax.axis_index("tensor").astype(jnp.int32)
    owner = lax.bitwise_xor(lax.rem(me + offset, NZ), flip)
    return up.at[pl.ds(pl.multiple_of(owner * TOK, TOK), TOK), :]


def load_kernel(source, out, sem):
    copy = pltpu.make_async_copy(source, out, sem)
    copy.start()
    copy.wait()


def load(source):
    return pl.pallas_call(
        load_kernel,
        out_shape=jax.ShapeDtypeStruct(source.shape, source.dtype),
        in_specs=[whole(pltpu.HBM)],
        out_specs=whole(VMEM),
        scratch_shapes=[pltpu.SemaphoreType.DMA],
        compiler_params=params(16),
        cost_estimate=cost(0, 3 << 20),
        name="load",
    )(pltpu.with_memory_space_constraint(source, pltpu.HBM))


def reply_kernel(near, across, tokens, *outs):
    low = lax.broadcasted_iota(jnp.int32, (TOK, BW), 1) < BH
    for i, out in enumerate(outs):
        halves = []
        for k in range(K):
            asked = (near if i < 2 else across)[(i % 2) * K + k]
            row = lax.shift_right_logical(jnp.maximum(asked, 0), 3)
            start = pl.multiple_of(lax.shift_right_logical(row, 1) * BW, BW)
            pair = tokens[:, pl.ds(start, BW)].astype(F32)
            turned = pltpu.roll(pair, BH, 1)
            halves.append(jnp.where(lax.bitwise_and(row, 1) == k, pair, turned))
        out[...] = jnp.where(low, halves[0], halves[1]).astype(BF16)


def reply(near, across, tokens):
    return pl.pallas_call(
        reply_kernel,
        out_shape=[jax.ShapeDtypeStruct((TOK, K * BH), BF16)] * NZ,
        in_specs=[whole(SMEM), whole(SMEM), whole(VMEM)],
        out_specs=[whole(VMEM)] * NZ,
        compiler_params=params(4),
        cost_estimate=cost(0, 1 << 20),
        name="reply",
    )(near, across, tokens)


def pick_kernel(chosen, up, fb, own, c1, c2, c3, out, block, sem):
    def fetch(k):
        number = jnp.maximum(chosen[k], 0)
        row = pl.multiple_of(lax.shift_right_logical(number, 3) * BH, BH)
        col = pl.multiple_of(lax.bitwise_and(number, 7) * BW, BW)
        return pltpu.make_async_copy(
            fb.at[pl.ds(row, BH), pl.ds(col, BW)], block.at[k], sem.at[k]
        )

    for k in range(K):
        fetch(k).start()
    lane = lax.broadcasted_iota(jnp.int32, (NOTE, BW), 1)
    out[K * BH :, :] = jnp.where(lane == 0, chosen[0], chosen[1]).astype(F32).astype(BF16)
    for k in range(K):
        col = pl.multiple_of(lax.bitwise_and(jnp.maximum(chosen[k], 0), 7) * BW, BW)
        total = jnp.zeros((K * BH, BW), F32)
        for flip, ref in zip(FLIPS, (own, c1, c2, c3)):
            total += lax.dot_general(
                ref[...],
                up_rows(up, flip=flip)[:, pl.ds(col, BW)],
                CONTRACT,
                preferred_element_type=F32,
            )
        fetch(k).wait()
        live = jnp.where(chosen[k] >= 0, 1.0, 0.0)
        value = total[k * BH : (k + 1) * BH] + block[k].astype(F32)
        out[k * BH : (k + 1) * BH, :] = (value * live).astype(BF16)


def pick(chosen, up, fb, parts):
    return pl.pallas_call(
        pick_kernel,
        out_shape=jax.ShapeDtypeStruct((K * BH + NOTE, BW), BF16),
        in_specs=[whole(SMEM), whole(VMEM), whole(pltpu.HBM)] + [whole(VMEM)] * NZ,
        out_specs=whole(VMEM),
        scratch_shapes=[VMEM((K, BH, BW), BF16), pltpu.SemaphoreType.DMA((K,))],
        compiler_params=params(40),
        cost_estimate=cost(2 * K * 128 * ROWS * BW, 2 << 20),
        name="pick",
    )(chosen, up, fb, *parts)


def old_moments(start, nxt, w1, w2, vals):
    def entry(i):
        slot = lax.shift_right_logical(i, 6)
        following = nxt[i]
        last = lax.shift_right_logical(following, 6) != slot
        value = vals[jnp.minimum(i, TOTAL - 1)].astype(F32)
        return slot, following, value, w1[slot], jnp.where(last, w2[slot], 0.0)

    def more(carry):
        return carry[0] < TOTAL

    def body(carry):
        i, before, m1, m2, acc = carry
        slot, following, value, one, two = entry(i)
        acc = value + jnp.where(slot == before, 1.0, 0.0) * acc
        return following, slot, m1 + one * value, m2 + two * acc * acc, acc

    slot, following, value, one, two = entry(start)
    carry = (following, slot, one * value, two * value * value, value)
    _, _, m1, m2, _ = lax.while_loop(more, body, carry)
    return m1, m2


def direction(m1, m2):
    return (m1 / (jnp.sqrt(m2) + epsilon)).astype(BF16)


WSTEP = 4
WPARTS = 2


def window_kernel(base, head, nxt, w1, w2, vals, *refs):
    out = refs[-1]
    first = (base + pl.program_id(0)) * WSTEP

    def row(q, _):
        place = pl.ds(pl.multiple_of(q * BH, BH), BH)
        for col in range(QS // BW):
            m1, m2 = old_moments(head[(first + q) * 8 + col], nxt, w1, w2, vals)
            out[place, col * BW : (col + 1) * BW] = direction(m1, m2)
        return 0

    lax.fori_loop(0, WSTEP, row, 0)


def window(part, head, nxt, w1, w2, vals, earlier):
    steps = D // BH // WSTEP // WPARTS
    base = part * steps
    extra = [] if earlier is None else [earlier]
    return pl.pallas_call(
        functools.partial(window_kernel, base),
        out_shape=jax.ShapeDtypeStruct((D, QS), BF16),
        grid=(steps,),
        in_specs=[whole(SMEM)] * 4 + [whole(VMEM)] + [whole(pl.ANY)] * len(extra),
        out_specs=pl.BlockSpec((WSTEP * BH, QS), lambda i: (base + i, 0)),
        input_output_aliases={5: 0} if extra else {},
        compiler_params=params(4),
        cost_estimate=cost(1e9, 10 << 20),
        name="window",
    )(head, nxt, w1, w2, vals, *extra)


def newest_kernel(
    head, old_nxt, w1, w2, got, vals, update, out, values,
    staged, listed, ids, nxt, first, seen, in_sem, out_sem,
):
    dp = lax.axis_index("dp").astype(jnp.int32)

    def order(r, _):
        place = place_of(lax.bitwise_xor(r, dp))
        for k in range(K):
            values[r * K + k] = got[place, k * BH : (k + 1) * BH]
        note = got[place, K * BH : K * BH + NOTE, :].astype(F32)
        listed[pl.ds(r, 1), :] = note[:1].astype(jnp.int32)
        return 0

    lax.fori_loop(0, N_DP, order, 0)
    fetch = pltpu.make_async_copy(listed, ids, in_sem)
    fetch.start()

    def clear(b, _):
        seen[b] = -1
        return 0

    lax.fori_loop(0, NBLK, clear, 0, unroll=8)
    fetch.wait()

    def number(e):
        return ids[lax.shift_right_logical(e, 1), lax.bitwise_and(e, 1)]

    def chain(e, _):
        block = number(e)
        nxt[e] = ENTRIES
        first[e] = 0

        @pl.when(block >= 0)
        def _():
            before = seen[block]
            seen[block] = e
            first[e] = jnp.where(before < 0, 1, 0)

            @pl.when(before >= 0)
            def _():
                nxt[before] = e

        return 0

    lax.fori_loop(0, ENTRIES, chain, 0)

    def out_copy(e):
        block = number(e)
        row = pl.multiple_of(lax.shift_right_logical(block, 3) * BH, BH)
        col = pl.multiple_of(lax.bitwise_and(block, 7) * BW, BW)
        return pltpu.make_async_copy(
            staged.at[e], out.at[pl.ds(row, BH), pl.ds(col, BW)], out_sem.at[e]
        )

    def finish(e, _):
        @pl.when(first[e] == 1)
        def _():
            def more(carry):
                return carry[0] < ENTRIES

            def body(carry):
                i, acc = carry
                return nxt[i], acc + values[i].astype(F32)

            m1, m2 = old_moments(head[number(e)], old_nxt, w1, w2, vals)
            _, acc = lax.while_loop(more, body, (nxt[e], values[e].astype(F32)))
            m1 = m1 + (1.0 - decay_first) * acc
            m2 = m2 + (1.0 - decay_second) * (acc * acc)
            staged[e] = direction(m1, m2)
            out_copy(e).start()

        return 0

    lax.fori_loop(0, ENTRIES, finish, 0)

    def drain(e, _):
        @pl.when(first[e] == 1)
        def _():
            out_copy(e).wait()

        return 0

    lax.fori_loop(0, ENTRIES, drain, 0)


def place_of(apart):
    core, y, x = apart & 1, (apart >> 1) & 3, (apart >> 3) & 3
    return core * 16 + (x ^ (x >> 1)) * 4 + (y ^ (y >> 1))


def newest(head, old_nxt, w1, w2, got, vals, update):
    return pl.pallas_call(
        newest_kernel,
        out_shape=(
            jax.ShapeDtypeStruct((D, QS), BF16),
            jax.ShapeDtypeStruct((ENTRIES, BH, BW), BF16),
        ),
        in_specs=[whole(SMEM)] * 4 + [whole(VMEM)] * 2 + [whole(pl.ANY)],
        out_specs=(whole(pl.ANY), whole(VMEM)),
        scratch_shapes=[
            VMEM((ENTRIES, BH, BW), BF16),
            VMEM((N_DP, BW), jnp.int32),
            SMEM((N_DP, BW), jnp.int32),
            SMEM((ENTRIES,), jnp.int32),
            SMEM((ENTRIES,), jnp.int32),
            SMEM((NBLK,), jnp.int32),
            pltpu.SemaphoreType.DMA,
            pltpu.SemaphoreType.DMA((ENTRIES,)),
        ],
        input_output_aliases={6: 0},
        compiler_params=params(4),
        cost_estimate=cost(1e9, 8 << 20),
        name="newest",
    )(head, old_nxt, w1, w2, got, vals, update)


ACC = jax.ShapeDtypeStruct((QUARTER, QS), F32)


def product(tokens, up):
    return lax.dot_general(tokens, up, CONTRACT, preferred_element_type=F32)


def middle_kernel(jobs, n_pieces, up, fb, *refs):
    pieces, outs = refs[:n_pieces], refs[n_pieces:]
    for (q, parts), out in zip(jobs, outs):
        total = fb[q * QUARTER : (q + 1) * QUARTER, :].astype(F32)
        for piece, at, offset in parts:
            tokens = pieces[piece][:, at * QUARTER : (at + 1) * QUARTER]
            total += product(tokens, up_rows(up, offset)[...])
        out[...] = total


def middle(up, fb, pieces, jobs):
    return pl.pallas_call(
        functools.partial(middle_kernel, jobs, len(pieces)),
        out_shape=[ACC] * len(jobs),
        in_specs=[whole(VMEM)] * (2 + len(pieces)),
        out_specs=[whole(VMEM)] * len(jobs),
        compiler_params=params(8),
        cost_estimate=cost(6 * TOK * QUARTER * QS * len(jobs), 4 << 20),
        name="middle",
    )(up, fb, *pieces)


NSPLIT = 4


def end_kernel(chosen, up, low, high, q0, q1, q2, q3, out, staged, sem):
    wide = QS // NSPLIT
    copies = []
    for q, acc in enumerate((q0, q1, q2, q3)):
        piece = (low if q < 2 else high)[:, (q % 2) * QUARTER : (q % 2 + 1) * QUARTER]
        for s in range(NSPLIT):
            cols = slice(s * wide, (s + 1) * wide)
            total = acc[:, cols] + product(piece, up_rows(up, 2)[:, cols])
            for r in range(QUARTER // BH):
                for c in range(wide // BW):
                    block = (q * QUARTER // BH + r) * 8 + s * (wide // BW) + c
                    cleared = (block == chosen[0]) | (block == chosen[1])
                    part = total[r * BH : (r + 1) * BH, c * BW : (c + 1) * BW]
                    staged[
                        q, r * BH : (r + 1) * BH, s * wide + c * BW : s * wide + (c + 1) * BW
                    ] = jnp.where(cleared, 0.0, part).astype(BF16)
            copies.append(
                pltpu.make_async_copy(
                    staged.at[q, :, cols],
                    out.at[q * QUARTER : (q + 1) * QUARTER, cols],
                    sem.at[q, s],
                )
            )
            copies[-1].start()
    for copy in copies:
        copy.wait()


def end(chosen, up, pieces, totals):
    return pl.pallas_call(
        end_kernel,
        out_shape=jax.ShapeDtypeStruct((D, QS), BF16),
        in_specs=[whole(SMEM)] + [whole(VMEM)] * 7,
        out_specs=whole(pl.ANY),
        scratch_shapes=[VMEM((4, QUARTER, QS), BF16), pltpu.SemaphoreType.DMA((4, NSPLIT))],
        compiler_params=params(8),
        cost_estimate=cost(2 * TOK * D * QS, 4 << 20),
        name="end",
    )(chosen, up, *pieces, *totals)


def after(value, *events):
    return lax.optimization_barrier((value, events))[0]


def local(
    activations, upstream_grad, feedback, selected, cycle_values, cycle_blocks, cycle_position
):
    a = activations[0]
    up = upstream_grad[0]
    fb = feedback[0]
    chosen = selected[0, 0]
    position = cycle_position[0]

    slots = jnp.arange(SLOTS)
    listed = jnp.where(slots[:, None] == position, -1, cycle_blocks.reshape(SLOTS, ENTRIES))
    listed = listed.reshape(-1)
    count = jnp.arange(TOTAL)
    place = jnp.arange(TOTAL + 128)
    row = jnp.concatenate([listed, jnp.full((128,), -2, jnp.int32)])
    later = (row[:, None] == listed[None, :]) & (count[None, :] > place[:, None])
    nxt = jnp.min(jnp.where(later, count[None, :], TOTAL), axis=1)
    here = jnp.arange(NBLK)[:, None] == listed[None, :]
    head = jnp.min(jnp.where(here, count[None, :], TOTAL), axis=1)
    table = jnp.arange(2 * SLOTS)
    age = jnp.mod(position - table, SLOTS).astype(F32)
    inside = table < SLOTS
    w1 = jnp.where(inside, (1.0 - decay_first) * jnp.power(decay_first, age), 0.0)
    w2 = jnp.where(inside, (1.0 - decay_second) * jnp.power(decay_second, age), 0.0)
    vals = cycle_values.reshape(TOTAL, BH, BW)

    known = swap(chosen, 1)
    across = pass_on(known, 3)
    tokens = load(a)

    parts = reply(known, across, tokens)
    replies = [pass_on(parts[i], flip) for i, flip in enumerate(FLIPS) if flip]
    low, high = after((tokens[:, :HALF], tokens[:, HALF:]), parts[0])
    right_0 = shift(low, "tensor", NZ, 1)
    left_0 = shift(high, "tensor", NZ, -1)
    fb_far = pltpu.with_memory_space_constraint(fb, pltpu.HBM)
    outgoing = pick(chosen, up, fb_far, [parts[0], *replies])
    vals = load(after(vals, outgoing))

    got_1 = dp_exchange(outgoing[None], lambda x, y, c: (x, y ^ 1, c))
    got_1 = after(got_1, vals)
    high_n, low_n = after((high, low), outgoing)
    rest_0 = shift(high_n, "tensor", NZ, 1)
    rest_1 = shift(low_n, "tensor", NZ, -1)
    update = window(0, after(head, got_1), nxt, w1, w2, vals, None)
    got_2 = dp_exchange(got_1, lambda x, y, c: (x, y ^ 3, c))
    got_2 = after(got_2, update)
    got_3 = dp_exchange(got_2, lambda x, y, c: (x ^ 1, y, c))
    far_0 = shift(after(right_0, left_0), "tensor", NZ, 1)
    far_1 = shift(after(left_0, right_0), "tensor", NZ, -1)
    got_3 = after(got_3, right_0, left_0)
    update = window(1, after(head, got_3), nxt, w1, w2, vals, update)
    got_4 = dp_exchange(got_3, lambda x, y, c: (x ^ 3, y, c))
    got = dp_exchange(after(got_4, update, rest_0, rest_1), lambda x, y, c: (x, y, c ^ 1))

    near = [tokens, right_0, left_0, rest_0, rest_1]
    totals = middle(
        up,
        fb,
        near,
        tuple(
            (q, ((0, q, 0), (1, q, 3), (4, q, 1)) if q < 2 else ((0, q, 0), (3, q - 2, 3), (2, q - 2, 1)))
            for q in range(4)
        ),
    )
    update_dir, newest_values = newest(head, nxt, w1, w2, got, vals, update)
    ready = after(chosen, newest_values)
    merged = end(ready, up, [far_0, far_1], totals)
    return (update_dir, merged[None], newest_values[None])


def solution(mesh):
    placed = (
        P("dp", "tensor", None),
        P("dp", None, "tensor"),
        P("dp", None, "tensor"),
        P("dp", "tensor", None),
        P(None, "tensor", None, None, None),
        P(None, "tensor", None),
        P(),
    )
    return jax.shard_map(
        local,
        mesh=mesh,
        in_specs=placed,
        out_specs=(P(None, "tensor"), P("dp", None, "tensor"), P("tensor", None, None, None)),
        check_vma=False,
    )
```

```python
import functools

import jax
import jax.numpy as jnp
from jax import lax
from jax.experimental import pallas as pl
from jax.experimental.pallas import tpu as pltpu
from jax.sharding import PartitionSpec as P

D = 2048
QS = 1024
BH = 64
BW = 128
K = 2
SLOTS = 8
NBLK = 256
ENTRIES = 64
NX = 4
NY = 4
NC = 2
NZ = 4
N_DP = 32
TOK = 384
ROWS = 1536
NOTE = 16
QUARTER = D // 4
HALF = D // 2
TOTAL = SLOTS * ENTRIES

decay_first = 0.9
decay_second = 0.999
epsilon = 0.001

CONTRACT = (((0,), (0,)), ((), ()))
SMEM = pltpu.SMEM
VMEM = pltpu.VMEM
F32 = jnp.float32
BF16 = jnp.bfloat16


def whole(space):
    return pl.BlockSpec(memory_space=space)


def params(mb):
    return pltpu.CompilerParams(vmem_limit_bytes=mb << 20)


def cost(flops, moved):
    return pl.CostEstimate(flops=1, bytes_accessed=1, transcendentals=0)


def shift(x, axis, size, step):
    return lax.ppermute(x, axis, [(i, (i + step) % size) for i in range(size)])


FLIPS = (0, 1, 3, 2)


def pass_on(x, flip):
    return lax.ppermute(x, "tensor", [(i, i ^ flip) for i in range(NZ)])


def swap(x, flip):
    return jnp.concatenate([x, pass_on(x, flip)])


def dp_index(x, y, c):
    return (x * NY + y) * NC + c


def dp_exchange(value, partner, meanwhile=()):
    pairs = []
    for x in range(NX):
        for y in range(NY):
            for c in range(NC):
                pairs.append((dp_index(x, y, c), dp_index(*partner(x, y, c))))
    received = lax.ppermute(value, "dp", pairs)
    return jnp.concatenate([value, lax.optimization_barrier((received, meanwhile))[0]])


def up_rows(up, offset=0, flip=0):
    me = lax.axis_index("tensor").astype(jnp.int32)
    owner = lax.bitwise_xor(lax.rem(me + offset, NZ), flip)
    return up.at[pl.ds(pl.multiple_of(owner * TOK, TOK), TOK), :]


def load_kernel(source, out, sem):
    copy = pltpu.make_async_copy(source, out, sem)
    copy.start()
    copy.wait()


def load(source):
    return pl.pallas_call(
        load_kernel,
        out_shape=jax.ShapeDtypeStruct(source.shape, source.dtype),
        in_specs=[whole(pltpu.HBM)],
        out_specs=whole(VMEM),
        scratch_shapes=[pltpu.SemaphoreType.DMA],
        compiler_params=params(16),
        cost_estimate=cost(0, 3 << 20),
        name="load",
    )(pltpu.with_memory_space_constraint(source, pltpu.HBM))


def reply_kernel(near, across, tokens, *outs):
    low = lax.broadcasted_iota(jnp.int32, (TOK, BW), 1) < BH
    for i, out in enumerate(outs):
        halves = []
        for k in range(K):
            asked = (near if i < 2 else across)[(i % 2) * K + k]
            row = lax.shift_right_logical(jnp.maximum(asked, 0), 3)
            start = pl.multiple_of(lax.shift_right_logical(row, 1) * BW, BW)
            pair = tokens[:, pl.ds(start, BW)].astype(F32)
            turned = pltpu.roll(pair, BH, 1)
            halves.append(jnp.where(lax.bitwise_and(row, 1) == k, pair, turned))
        out[...] = jnp.where(low, halves[0], halves[1]).astype(BF16)


def reply(near, across, tokens):
    return pl.pallas_call(
        reply_kernel,
        out_shape=[jax.ShapeDtypeStruct((TOK, K * BH), BF16)] * NZ,
        in_specs=[whole(SMEM), whole(SMEM), whole(VMEM)],
        out_specs=[whole(VMEM)] * NZ,
        compiler_params=params(4),
        cost_estimate=cost(0, 1 << 20),
        name="reply",
    )(near, across, tokens)


def pick_kernel(chosen, up, fb, own, c1, c2, c3, out, block, sem):
    def fetch(k):
        number = jnp.maximum(chosen[k], 0)
        row = pl.multiple_of(lax.shift_right_logical(number, 3) * BH, BH)
        col = pl.multiple_of(lax.bitwise_and(number, 7) * BW, BW)
        return pltpu.make_async_copy(
            fb.at[pl.ds(row, BH), pl.ds(col, BW)], block.at[k], sem.at[k]
        )

    for k in range(K):
        fetch(k).start()
    lane = lax.broadcasted_iota(jnp.int32, (NOTE, BW), 1)
    out[K * BH :, :] = jnp.where(lane == 0, chosen[0], chosen[1]).astype(F32).astype(BF16)
    for k in range(K):
        col = pl.multiple_of(lax.bitwise_and(jnp.maximum(chosen[k], 0), 7) * BW, BW)
        total = jnp.zeros((K * BH, BW), F32)
        for flip, ref in zip(FLIPS, (own, c1, c2, c3)):
            total += lax.dot_general(
                ref[...],
                up_rows(up, flip=flip)[:, pl.ds(col, BW)],
                CONTRACT,
                preferred_element_type=F32,
            )
        fetch(k).wait()
        live = jnp.where(chosen[k] >= 0, 1.0, 0.0)
        value = total[k * BH : (k + 1) * BH] + block[k].astype(F32)
        out[k * BH : (k + 1) * BH, :] = (value * live).astype(BF16)


def pick(chosen, up, fb, parts):
    return pl.pallas_call(
        pick_kernel,
        out_shape=jax.ShapeDtypeStruct((K * BH + NOTE, BW), BF16),
        in_specs=[whole(SMEM), whole(VMEM), whole(pltpu.HBM)] + [whole(VMEM)] * NZ,
        out_specs=whole(VMEM),
        scratch_shapes=[VMEM((K, BH, BW), BF16), pltpu.SemaphoreType.DMA((K,))],
        compiler_params=params(40),
        cost_estimate=cost(2 * K * 128 * ROWS * BW, 2 << 20),
        name="pick",
    )(chosen, up, fb, *parts)


def old_moments(start, nxt, w1, w2, vals):
    def entry(i):
        slot = lax.shift_right_logical(i, 6)
        following = nxt[i]
        last = lax.shift_right_logical(following, 6) != slot
        value = vals[jnp.minimum(i, TOTAL - 1)].astype(F32)
        return slot, following, value, w1[slot], jnp.where(last, w2[slot], 0.0)

    def more(carry):
        return carry[0] < TOTAL

    def body(carry):
        i, before, m1, m2, acc = carry
        slot, following, value, one, two = entry(i)
        acc = value + jnp.where(slot == before, 1.0, 0.0) * acc
        return following, slot, m1 + one * value, m2 + two * acc * acc, acc

    slot, following, value, one, two = entry(start)
    carry = (following, slot, one * value, two * value * value, value)
    _, _, m1, m2, _ = lax.while_loop(more, body, carry)
    return m1, m2


def direction(m1, m2):
    return (m1 / (jnp.sqrt(m2) + epsilon)).astype(BF16)


WSTEP = 4
WPARTS = 2


def window_kernel(base, head, nxt, w1, w2, vals, *refs):
    out = refs[-1]
    first = (base + pl.program_id(0)) * WSTEP

    def row(q, _):
        place = pl.ds(pl.multiple_of(q * BH, BH), BH)
        for col in range(QS // BW):
            m1, m2 = old_moments(head[(first + q) * 8 + col], nxt, w1, w2, vals)
            out[place, col * BW : (col + 1) * BW] = direction(m1, m2)
        return 0

    lax.fori_loop(0, WSTEP, row, 0)


def window(part, head, nxt, w1, w2, vals, earlier):
    steps = D // BH // WSTEP // WPARTS
    base = part * steps
    extra = [] if earlier is None else [earlier]
    return pl.pallas_call(
        functools.partial(window_kernel, base),
        out_shape=jax.ShapeDtypeStruct((D, QS), BF16),
        grid=(steps,),
        in_specs=[whole(SMEM)] * 4 + [whole(VMEM)] + [whole(pl.ANY)] * len(extra),
        out_specs=pl.BlockSpec((WSTEP * BH, QS), lambda i: (base + i, 0)),
        input_output_aliases={5: 0} if extra else {},
        compiler_params=params(4),
        cost_estimate=cost(1e9, 10 << 20),
        name="window",
    )(head, nxt, w1, w2, vals, *extra)


def newest_kernel(
    head, old_nxt, w1, w2, got, vals, update, out, values,
    staged, listed, ids, nxt, first, seen, in_sem, out_sem,
):
    dp = lax.axis_index("dp").astype(jnp.int32)

    def order(r, _):
        place = place_of(lax.bitwise_xor(r, dp))
        for k in range(K):
            values[r * K + k] = got[place, k * BH : (k + 1) * BH]
        note = got[place, K * BH : K * BH + NOTE, :].astype(F32)
        listed[pl.ds(r, 1), :] = note[:1].astype(jnp.int32)
        return 0

    lax.fori_loop(0, N_DP, order, 0)
    fetch = pltpu.make_async_copy(listed, ids, in_sem)
    fetch.start()

    def clear(b, _):
        seen[b] = -1
        return 0

    lax.fori_loop(0, NBLK, clear, 0, unroll=8)
    fetch.wait()

    def number(e):
        return ids[lax.shift_right_logical(e, 1), lax.bitwise_and(e, 1)]

    def chain(e, _):
        block = number(e)
        nxt[e] = ENTRIES
        first[e] = 0

        @pl.when(block >= 0)
        def _():
            before = seen[block]
            seen[block] = e
            first[e] = jnp.where(before < 0, 1, 0)

            @pl.when(before >= 0)
            def _():
                nxt[before] = e

        return 0

    lax.fori_loop(0, ENTRIES, chain, 0)

    def out_copy(e):
        block = number(e)
        row = pl.multiple_of(lax.shift_right_logical(block, 3) * BH, BH)
        col = pl.multiple_of(lax.bitwise_and(block, 7) * BW, BW)
        return pltpu.make_async_copy(
            staged.at[e], out.at[pl.ds(row, BH), pl.ds(col, BW)], out_sem.at[e]
        )

    def finish(e, _):
        @pl.when(first[e] == 1)
        def _():
            def more(carry):
                return carry[0] < ENTRIES

            def body(carry):
                i, acc = carry
                return nxt[i], acc + values[i].astype(F32)

            m1, m2 = old_moments(head[number(e)], old_nxt, w1, w2, vals)
            _, acc = lax.while_loop(more, body, (nxt[e], values[e].astype(F32)))
            m1 = m1 + (1.0 - decay_first) * acc
            m2 = m2 + (1.0 - decay_second) * (acc * acc)
            staged[e] = direction(m1, m2)
            out_copy(e).start()

        return 0

    lax.fori_loop(0, ENTRIES, finish, 0)

    def drain(e, _):
        @pl.when(first[e] == 1)
        def _():
            out_copy(e).wait()

        return 0

    lax.fori_loop(0, ENTRIES, drain, 0)


def place_of(apart):
    core, y, x = apart & 1, (apart >> 1) & 3, (apart >> 3) & 3
    return core * 16 + (x ^ (x >> 1)) * 4 + (y ^ (y >> 1))


def newest(head, old_nxt, w1, w2, got, vals, update):
    return pl.pallas_call(
        newest_kernel,
        out_shape=(
            jax.ShapeDtypeStruct((D, QS), BF16),
            jax.ShapeDtypeStruct((ENTRIES, BH, BW), BF16),
        ),
        in_specs=[whole(SMEM)] * 4 + [whole(VMEM)] * 2 + [whole(pl.ANY)],
        out_specs=(whole(pl.ANY), whole(VMEM)),
        scratch_shapes=[
            VMEM((ENTRIES, BH, BW), BF16),
            VMEM((N_DP, BW), jnp.int32),
            SMEM((N_DP, BW), jnp.int32),
            SMEM((ENTRIES,), jnp.int32),
            SMEM((ENTRIES,), jnp.int32),
            SMEM((NBLK,), jnp.int32),
            pltpu.SemaphoreType.DMA,
            pltpu.SemaphoreType.DMA((ENTRIES,)),
        ],
        input_output_aliases={6: 0},
        compiler_params=params(4),
        cost_estimate=cost(1e9, 8 << 20),
        name="newest",
    )(head, old_nxt, w1, w2, got, vals, update)


ACC = jax.ShapeDtypeStruct((QUARTER, QS), F32)


def product(tokens, up):
    return lax.dot_general(tokens, up, CONTRACT, preferred_element_type=F32)


def first_kernel(up, fb, tokens, right, left, *outs):
    for q, out in enumerate(outs):
        part = slice(q * QUARTER, (q + 1) * QUARTER)
        total = fb[part, :].astype(F32) + product(tokens[:, part], up_rows(up)[...])
        piece, offset = (right, 3) if q < 2 else (left, 1)
        half = slice((q % 2) * QUARTER, (q % 2 + 1) * QUARTER)
        out[...] = total + product(piece[:, half], up_rows(up, offset)[...])


def first_products(up, fb, tokens, right, left):
    return pl.pallas_call(
        first_kernel,
        out_shape=[ACC] * 4,
        in_specs=[whole(VMEM)] * 5,
        out_specs=[whole(VMEM)] * 4,
        compiler_params=params(8),
        cost_estimate=cost(4 * TOK * D * QS, 4 << 20),
        name="first_products",
    )(up, fb, tokens, right, left)


def second_kernel(up, right, left, q0, q1, q2, q3, *outs):
    for q, (acc, out) in enumerate(zip((q0, q1, q2, q3), outs)):
        piece, offset = (left, 1) if q < 2 else (right, 3)
        half = slice((q % 2) * QUARTER, (q % 2 + 1) * QUARTER)
        out[...] = acc[...] + product(piece[:, half], up_rows(up, offset)[...])


def second_products(up, right, left, totals):
    return pl.pallas_call(
        second_kernel,
        out_shape=[ACC] * 4,
        in_specs=[whole(VMEM)] * 7,
        out_specs=[whole(VMEM)] * 4,
        input_output_aliases={3 + i: i for i in range(4)},
        compiler_params=params(8),
        cost_estimate=cost(2 * TOK * D * QS, 4 << 20),
        name="second_products",
    )(up, right, left, *totals)


NSPLIT = 2


def end_kernel(chosen, up, low, high, q0, q1, q2, q3, out, staged, sem):
    wide = QS // NSPLIT
    copies = []
    for q, acc in enumerate((q0, q1, q2, q3)):
        piece = (low if q < 2 else high)[:, (q % 2) * QUARTER : (q % 2 + 1) * QUARTER]
        for s in range(NSPLIT):
            cols = slice(s * wide, (s + 1) * wide)
            total = acc[:, cols] + product(piece, up_rows(up, 2)[:, cols])
            for r in range(QUARTER // BH):
                for c in range(wide // BW):
                    block = (q * QUARTER // BH + r) * 8 + s * (wide // BW) + c
                    cleared = (block == chosen[0]) | (block == chosen[1])
                    part = total[r * BH : (r + 1) * BH, c * BW : (c + 1) * BW]
                    staged[
                        q, r * BH : (r + 1) * BH, s * wide + c * BW : s * wide + (c + 1) * BW
                    ] = jnp.where(cleared, 0.0, part).astype(BF16)
            copies.append(
                pltpu.make_async_copy(
                    staged.at[q, :, cols],
                    out.at[q * QUARTER : (q + 1) * QUARTER, cols],
                    sem.at[q, s],
                )
            )
            copies[-1].start()
    for copy in copies:
        copy.wait()


def end(chosen, up, pieces, totals):
    return pl.pallas_call(
        end_kernel,
        out_shape=jax.ShapeDtypeStruct((D, QS), BF16),
        in_specs=[whole(SMEM)] + [whole(VMEM)] * 7,
        out_specs=whole(pl.ANY),
        scratch_shapes=[VMEM((4, QUARTER, QS), BF16), pltpu.SemaphoreType.DMA((4, NSPLIT))],
        compiler_params=params(8),
        cost_estimate=cost(2 * TOK * D * QS, 4 << 20),
        name="end",
    )(chosen, up, *pieces, *totals)


def after(value, *events):
    return lax.optimization_barrier((value, events))[0]


def local(
    activations, upstream_grad, feedback, selected, cycle_values, cycle_blocks, cycle_position
):
    a = activations[0]
    up = upstream_grad[0]
    fb = feedback[0]
    chosen = selected[0, 0]
    position = cycle_position[0]

    slots = jnp.arange(SLOTS)
    listed = jnp.where(slots[:, None] == position, -1, cycle_blocks.reshape(SLOTS, ENTRIES))
    listed = listed.reshape(-1)
    count = jnp.arange(TOTAL)
    place = jnp.arange(TOTAL + 128)
    row = jnp.concatenate([listed, jnp.full((128,), -2, jnp.int32)])
    later = (row[:, None] == listed[None, :]) & (count[None, :] > place[:, None])
    nxt = jnp.min(jnp.where(later, count[None, :], TOTAL), axis=1)
    here = jnp.arange(NBLK)[:, None] == listed[None, :]
    head = jnp.min(jnp.where(here, count[None, :], TOTAL), axis=1)
    table = jnp.arange(2 * SLOTS)
    age = jnp.mod(position - table, SLOTS).astype(F32)
    inside = table < SLOTS
    w1 = jnp.where(inside, (1.0 - decay_first) * jnp.power(decay_first, age), 0.0)
    w2 = jnp.where(inside, (1.0 - decay_second) * jnp.power(decay_second, age), 0.0)
    vals = cycle_values.reshape(TOTAL, BH, BW)

    known = swap(chosen, 1)
    across = pass_on(known, 3)
    tokens = load(a)

    parts = reply(known, across, tokens)
    replies = [pass_on(parts[i], flip) for i, flip in enumerate(FLIPS) if flip]
    low, high = after((tokens[:, :HALF], tokens[:, HALF:]), parts[0])
    right_0 = shift(low, "tensor", NZ, 1)
    left_0 = shift(high, "tensor", NZ, -1)
    fb_far = pltpu.with_memory_space_constraint(fb, pltpu.HBM)
    outgoing = pick(chosen, up, fb_far, [parts[0], *replies])
    vals = load(after(vals, outgoing))
    got_1 = dp_exchange(outgoing[None], lambda x, y, c: (x, y ^ 1, c), vals)
    high_n, low_n = after((high, low), outgoing)
    rest_0 = shift(high_n, "tensor", NZ, 1)
    rest_1 = shift(low_n, "tensor", NZ, -1)
    update = window(0, after(head, got_1), nxt, w1, w2, vals, None)
    got_2 = dp_exchange(got_1, lambda x, y, c: (x, y ^ 3, c), update)
    totals = first_products(up, after(fb, got_2), tokens, right_0, left_0)
    got_3 = dp_exchange(got_2, lambda x, y, c: (x ^ 1, y, c), totals)
    far_0 = shift(after(right_0, left_0), "tensor", NZ, 1)
    far_1 = shift(after(left_0, right_0), "tensor", NZ, -1)
    update = window(1, after(head, got_3), nxt, w1, w2, vals, update)
    got_4 = dp_exchange(got_3, lambda x, y, c: (x ^ 3, y, c), (update, rest_0, rest_1))
    totals = second_products(up, after(rest_0, got_4), rest_1, totals)
    got = dp_exchange(got_4, lambda x, y, c: (x, y, c ^ 1), totals)
    update_dir, newest_values = newest(head, nxt, w1, w2, got, vals, update)
    ready = after(chosen, newest_values)
    merged = end(ready, up, [far_0, far_1], totals)
    return (update_dir, merged[None], newest_values[None])


def solution(mesh):
    placed = (
        P("dp", "tensor", None),
        P("dp", None, "tensor"),
        P("dp", None, "tensor"),
        P("dp", "tensor", None),
        P(None, "tensor", None, None, None),
        P(None, "tensor", None),
        P(),
    )
    return jax.shard_map(
        local,
        mesh=mesh,
        in_specs=placed,
        out_specs=(P(None, "tensor"), P("dp", None, "tensor"), P("tensor", None, None, None)),
        check_vma=False,
    )
```

```python
import functools

import jax
import jax.numpy as jnp
from jax import lax
from jax.experimental import pallas as pl
from jax.experimental.pallas import tpu as pltpu
from jax.sharding import PartitionSpec as P

D = 2048
QS = 1024
BH = 64
BW = 128
K = 2
SLOTS = 8
NBLK = 256
ENTRIES = 64
NX = 4
NY = 4
NC = 2
NZ = 4
N_DP = 32
TOK = 384
ROWS = 1536
NOTE = 16
QUARTER = D // 4
HALF = D // 2
TOTAL = SLOTS * ENTRIES

decay_first = 0.9
decay_second = 0.999
epsilon = 0.001

CONTRACT = (((0,), (0,)), ((), ()))
SMEM = pltpu.SMEM
VMEM = pltpu.VMEM
F32 = jnp.float32
BF16 = jnp.bfloat16


def whole(space):
    return pl.BlockSpec(memory_space=space)


def params(mb):
    return pltpu.CompilerParams(vmem_limit_bytes=mb << 20)


def cost(flops, moved):
    return pl.CostEstimate(flops=1, bytes_accessed=1, transcendentals=0)


def shift(x, axis, size, step):
    return lax.ppermute(x, axis, [(i, (i + step) % size) for i in range(size)])


FLIPS = (0, 1, 3, 2)


def pass_on(x, flip):
    return lax.ppermute(x, "tensor", [(i, i ^ flip) for i in range(NZ)])


def swap(x, flip):
    return jnp.concatenate([x, pass_on(x, flip)])


def dp_index(x, y, c):
    return (x * NY + y) * NC + c


def dp_exchange(value, partner, meanwhile=()):
    pairs = []
    for x in range(NX):
        for y in range(NY):
            for c in range(NC):
                pairs.append((dp_index(x, y, c), dp_index(*partner(x, y, c))))
    received = lax.ppermute(value, "dp", pairs)
    return jnp.concatenate([value, lax.optimization_barrier((received, meanwhile))[0]])


def up_rows(up, offset=0, flip=0):
    me = lax.axis_index("tensor").astype(jnp.int32)
    owner = lax.bitwise_xor(lax.rem(me + offset, NZ), flip)
    return up.at[pl.ds(pl.multiple_of(owner * TOK, TOK), TOK), :]


def load_kernel(source, out, sem):
    copy = pltpu.make_async_copy(source, out, sem)
    copy.start()
    copy.wait()


def load(source):
    return pl.pallas_call(
        load_kernel,
        out_shape=jax.ShapeDtypeStruct(source.shape, source.dtype),
        in_specs=[whole(pltpu.HBM)],
        out_specs=whole(VMEM),
        scratch_shapes=[pltpu.SemaphoreType.DMA],
        compiler_params=params(16),
        cost_estimate=cost(0, 3 << 20),
        name="load",
    )(pltpu.with_memory_space_constraint(source, pltpu.HBM))


def reply_kernel(near, across, tokens, *outs):
    low = lax.broadcasted_iota(jnp.int32, (TOK, BW), 1) < BH
    for i, out in enumerate(outs):
        halves = []
        for k in range(K):
            asked = (near if i < 2 else across)[(i % 2) * K + k]
            row = lax.shift_right_logical(jnp.maximum(asked, 0), 3)
            start = pl.multiple_of(lax.shift_right_logical(row, 1) * BW, BW)
            pair = tokens[:, pl.ds(start, BW)].astype(F32)
            turned = pltpu.roll(pair, BH, 1)
            halves.append(jnp.where(lax.bitwise_and(row, 1) == k, pair, turned))
        out[...] = jnp.where(low, halves[0], halves[1]).astype(BF16)


def reply(near, across, tokens):
    return pl.pallas_call(
        reply_kernel,
        out_shape=[jax.ShapeDtypeStruct((TOK, K * BH), BF16)] * NZ,
        in_specs=[whole(SMEM), whole(SMEM), whole(VMEM)],
        out_specs=[whole(VMEM)] * NZ,
        compiler_params=params(4),
        cost_estimate=cost(0, 1 << 20),
        name="reply",
    )(near, across, tokens)


def pick_kernel(chosen, up, fb, own, c1, c2, c3, out, block, sem):
    def fetch(k):
        number = jnp.maximum(chosen[k], 0)
        row = pl.multiple_of(lax.shift_right_logical(number, 3) * BH, BH)
        col = pl.multiple_of(lax.bitwise_and(number, 7) * BW, BW)
        return pltpu.make_async_copy(
            fb.at[pl.ds(row, BH), pl.ds(col, BW)], block.at[k], sem.at[k]
        )

    for k in range(K):
        fetch(k).start()
    lane = lax.broadcasted_iota(jnp.int32, (NOTE, BW), 1)
    out[K * BH :, :] = jnp.where(lane == 0, chosen[0], chosen[1]).astype(F32).astype(BF16)
    for k in range(K):
        col = pl.multiple_of(lax.bitwise_and(jnp.maximum(chosen[k], 0), 7) * BW, BW)
        total = jnp.zeros((K * BH, BW), F32)
        for flip, ref in zip(FLIPS, (own, c1, c2, c3)):
            total += lax.dot_general(
                ref[...],
                up_rows(up, flip=flip)[:, pl.ds(col, BW)],
                CONTRACT,
                preferred_element_type=F32,
            )
        fetch(k).wait()
        live = jnp.where(chosen[k] >= 0, 1.0, 0.0)
        value = total[k * BH : (k + 1) * BH] + block[k].astype(F32)
        out[k * BH : (k + 1) * BH, :] = (value * live).astype(BF16)


def pick(chosen, up, fb, parts):
    return pl.pallas_call(
        pick_kernel,
        out_shape=jax.ShapeDtypeStruct((K * BH + NOTE, BW), BF16),
        in_specs=[whole(SMEM), whole(VMEM), whole(pltpu.HBM)] + [whole(VMEM)] * NZ,
        out_specs=whole(VMEM),
        scratch_shapes=[VMEM((K, BH, BW), BF16), pltpu.SemaphoreType.DMA((K,))],
        compiler_params=params(40),
        cost_estimate=cost(2 * K * 128 * ROWS * BW, 2 << 20),
        name="pick",
    )(chosen, up, fb, *parts)


def old_moments(start, nxt, w1, w2, vals):
    def entry(i):
        slot = lax.shift_right_logical(i, 6)
        following = nxt[i]
        last = lax.shift_right_logical(following, 6) != slot
        value = vals[jnp.minimum(i, TOTAL - 1)].astype(F32)
        return slot, following, value, w1[slot], jnp.where(last, w2[slot], 0.0)

    def more(carry):
        return carry[0] < TOTAL

    def body(carry):
        i, before, m1, m2, acc = carry
        slot, following, value, one, two = entry(i)
        acc = value + jnp.where(slot == before, 1.0, 0.0) * acc
        return following, slot, m1 + one * value, m2 + two * acc * acc, acc

    slot, following, value, one, two = entry(start)
    carry = (following, slot, one * value, two * value * value, value)
    _, _, m1, m2, _ = lax.while_loop(more, body, carry)
    return m1, m2


def direction(m1, m2):
    return (m1 / (jnp.sqrt(m2) + epsilon)).astype(BF16)


WSTEP = 4
WPARTS = 2


def window_kernel(base, head, nxt, w1, w2, vals, *refs):
    out = refs[-1]
    first = (base + pl.program_id(0)) * WSTEP

    def row(q, _):
        place = pl.ds(pl.multiple_of(q * BH, BH), BH)
        for col in range(QS // BW):
            m1, m2 = old_moments(head[(first + q) * 8 + col], nxt, w1, w2, vals)
            out[place, col * BW : (col + 1) * BW] = direction(m1, m2)
        return 0

    lax.fori_loop(0, WSTEP, row, 0)


def window(part, head, nxt, w1, w2, vals, earlier):
    steps = D // BH // WSTEP // WPARTS
    base = part * steps
    extra = [] if earlier is None else [earlier]
    return pl.pallas_call(
        functools.partial(window_kernel, base),
        out_shape=jax.ShapeDtypeStruct((D, QS), BF16),
        grid=(steps,),
        in_specs=[whole(SMEM)] * 4 + [whole(VMEM)] + [whole(pl.ANY)] * len(extra),
        out_specs=pl.BlockSpec((WSTEP * BH, QS), lambda i: (base + i, 0)),
        input_output_aliases={5: 0} if extra else {},
        compiler_params=params(4),
        cost_estimate=cost(1e9, 10 << 20),
        name="window",
    )(head, nxt, w1, w2, vals, *extra)


def newest_kernel(
    head, old_nxt, w1, w2, got, vals, update, out, values,
    staged, listed, ids, nxt, first, seen, in_sem, out_sem,
):
    dp = lax.axis_index("dp").astype(jnp.int32)

    def order(r, _):
        place = place_of(lax.bitwise_xor(r, dp))
        for k in range(K):
            values[r * K + k] = got[place, k * BH : (k + 1) * BH]
        note = got[place, K * BH : K * BH + NOTE, :].astype(F32)
        listed[pl.ds(r, 1), :] = note[:1].astype(jnp.int32)
        return 0

    lax.fori_loop(0, N_DP, order, 0)
    fetch = pltpu.make_async_copy(listed, ids, in_sem)
    fetch.start()

    def clear(b, _):
        seen[b] = -1
        return 0

    lax.fori_loop(0, NBLK, clear, 0, unroll=8)
    fetch.wait()

    def number(e):
        return ids[lax.shift_right_logical(e, 1), lax.bitwise_and(e, 1)]

    def chain(e, _):
        block = number(e)
        nxt[e] = ENTRIES
        first[e] = 0

        @pl.when(block >= 0)
        def _():
            before = seen[block]
            seen[block] = e
            first[e] = jnp.where(before < 0, 1, 0)

            @pl.when(before >= 0)
            def _():
                nxt[before] = e

        return 0

    lax.fori_loop(0, ENTRIES, chain, 0)

    def out_copy(e):
        block = number(e)
        row = pl.multiple_of(lax.shift_right_logical(block, 3) * BH, BH)
        col = pl.multiple_of(lax.bitwise_and(block, 7) * BW, BW)
        return pltpu.make_async_copy(
            staged.at[e], out.at[pl.ds(row, BH), pl.ds(col, BW)], out_sem.at[e]
        )

    def finish(e, _):
        @pl.when(first[e] == 1)
        def _():
            def more(carry):
                return carry[0] < ENTRIES

            def body(carry):
                i, acc = carry
                return nxt[i], acc + values[i].astype(F32)

            m1, m2 = old_moments(head[number(e)], old_nxt, w1, w2, vals)
            _, acc = lax.while_loop(more, body, (nxt[e], values[e].astype(F32)))
            m1 = m1 + (1.0 - decay_first) * acc
            m2 = m2 + (1.0 - decay_second) * (acc * acc)
            staged[e] = direction(m1, m2)
            out_copy(e).start()

        return 0

    lax.fori_loop(0, ENTRIES, finish, 0)

    def drain(e, _):
        @pl.when(first[e] == 1)
        def _():
            out_copy(e).wait()

        return 0

    lax.fori_loop(0, ENTRIES, drain, 0)


def place_of(apart):
    core, y, x = apart & 1, (apart >> 1) & 3, (apart >> 3) & 3
    return core * 16 + (x ^ (x >> 1)) * 4 + (y ^ (y >> 1))


def newest(head, old_nxt, w1, w2, got, vals, update):
    return pl.pallas_call(
        newest_kernel,
        out_shape=(
            jax.ShapeDtypeStruct((D, QS), BF16),
            jax.ShapeDtypeStruct((ENTRIES, BH, BW), BF16),
        ),
        in_specs=[whole(SMEM)] * 4 + [whole(VMEM)] * 2 + [whole(pl.ANY)],
        out_specs=(whole(pl.ANY), whole(VMEM)),
        scratch_shapes=[
            VMEM((ENTRIES, BH, BW), BF16),
            VMEM((N_DP, BW), jnp.int32),
            SMEM((N_DP, BW), jnp.int32),
            SMEM((ENTRIES,), jnp.int32),
            SMEM((ENTRIES,), jnp.int32),
            SMEM((NBLK,), jnp.int32),
            pltpu.SemaphoreType.DMA,
            pltpu.SemaphoreType.DMA((ENTRIES,)),
        ],
        input_output_aliases={6: 0},
        compiler_params=params(4),
        cost_estimate=cost(1e9, 8 << 20),
        name="newest",
    )(head, old_nxt, w1, w2, got, vals, update)


ACC = jax.ShapeDtypeStruct((QUARTER, QS), F32)


def product(tokens, up):
    return lax.dot_general(tokens, up, CONTRACT, preferred_element_type=F32)


def first_kernel(up, fb, tokens, right, left, *outs):
    for q, out in enumerate(outs):
        part = slice(q * QUARTER, (q + 1) * QUARTER)
        total = fb[part, :].astype(F32) + product(tokens[:, part], up_rows(up)[...])
        piece, offset = (right, 3) if q < 2 else (left, 1)
        half = slice((q % 2) * QUARTER, (q % 2 + 1) * QUARTER)
        out[...] = total + product(piece[:, half], up_rows(up, offset)[...])


def first_products(up, fb, tokens, right, left):
    return pl.pallas_call(
        first_kernel,
        out_shape=[ACC] * 4,
        in_specs=[whole(VMEM)] * 5,
        out_specs=[whole(VMEM)] * 4,
        compiler_params=params(8),
        cost_estimate=cost(4 * TOK * D * QS, 4 << 20),
        name="first_products",
    )(up, fb, tokens, right, left)


def second_kernel(up, right, left, q0, q1, q2, q3, *outs):
    for q, (acc, out) in enumerate(zip((q0, q1, q2, q3), outs)):
        piece, offset = (left, 1) if q < 2 else (right, 3)
        half = slice((q % 2) * QUARTER, (q % 2 + 1) * QUARTER)
        out[...] = acc[...] + product(piece[:, half], up_rows(up, offset)[...])


def second_products(up, right, left, totals):
    return pl.pallas_call(
        second_kernel,
        out_shape=[ACC] * 4,
        in_specs=[whole(VMEM)] * 7,
        out_specs=[whole(VMEM)] * 4,
        input_output_aliases={3 + i: i for i in range(4)},
        compiler_params=params(8),
        cost_estimate=cost(2 * TOK * D * QS, 4 << 20),
        name="second_products",
    )(up, right, left, *totals)


NSPLIT = 1


def end_kernel(chosen, up, low, high, q0, q1, q2, q3, out, staged, sem):
    wide = QS // NSPLIT
    copies = []
    for q, acc in enumerate((q0, q1, q2, q3)):
        piece = (low if q < 2 else high)[:, (q % 2) * QUARTER : (q % 2 + 1) * QUARTER]
        for s in range(NSPLIT):
            cols = slice(s * wide, (s + 1) * wide)
            total = acc[:, cols] + product(piece, up_rows(up, 2)[:, cols])
            for r in range(QUARTER // BH):
                for c in range(wide // BW):
                    block = (q * QUARTER // BH + r) * 8 + s * (wide // BW) + c
                    cleared = (block == chosen[0]) | (block == chosen[1])
                    part = total[r * BH : (r + 1) * BH, c * BW : (c + 1) * BW]
                    staged[
                        q, r * BH : (r + 1) * BH, s * wide + c * BW : s * wide + (c + 1) * BW
                    ] = jnp.where(cleared, 0.0, part).astype(BF16)
            copies.append(
                pltpu.make_async_copy(
                    staged.at[q, :, cols],
                    out.at[q * QUARTER : (q + 1) * QUARTER, cols],
                    sem.at[q, s],
                )
            )
            copies[-1].start()
    for copy in copies:
        copy.wait()


def end(chosen, up, pieces, totals):
    return pl.pallas_call(
        end_kernel,
        out_shape=jax.ShapeDtypeStruct((D, QS), BF16),
        in_specs=[whole(SMEM)] + [whole(VMEM)] * 7,
        out_specs=whole(pl.ANY),
        scratch_shapes=[VMEM((4, QUARTER, QS), BF16), pltpu.SemaphoreType.DMA((4, NSPLIT))],
        compiler_params=params(8),
        cost_estimate=cost(2 * TOK * D * QS, 4 << 20),
        name="end",
    )(chosen, up, *pieces, *totals)


def after(value, *events):
    return lax.optimization_barrier((value, events))[0]


def local(
    activations, upstream_grad, feedback, selected, cycle_values, cycle_blocks, cycle_position
):
    a = activations[0]
    up = upstream_grad[0]
    fb = feedback[0]
    chosen = selected[0, 0]
    position = cycle_position[0]

    slots = jnp.arange(SLOTS)
    listed = jnp.where(slots[:, None] == position, -1, cycle_blocks.reshape(SLOTS, ENTRIES))
    listed = listed.reshape(-1)
    count = jnp.arange(TOTAL)
    place = jnp.arange(TOTAL + 128)
    row = jnp.concatenate([listed, jnp.full((128,), -2, jnp.int32)])
    later = (row[:, None] == listed[None, :]) & (count[None, :] > place[:, None])
    nxt = jnp.min(jnp.where(later, count[None, :], TOTAL), axis=1)
    here = jnp.arange(NBLK)[:, None] == listed[None, :]
    head = jnp.min(jnp.where(here, count[None, :], TOTAL), axis=1)
    table = jnp.arange(2 * SLOTS)
    age = jnp.mod(position - table, SLOTS).astype(F32)
    inside = table < SLOTS
    w1 = jnp.where(inside, (1.0 - decay_first) * jnp.power(decay_first, age), 0.0)
    w2 = jnp.where(inside, (1.0 - decay_second) * jnp.power(decay_second, age), 0.0)
    vals = cycle_values.reshape(TOTAL, BH, BW)

    known = swap(chosen, 1)
    across = pass_on(known, 3)
    tokens = load(a)

    parts = reply(known, across, tokens)
    replies = [pass_on(parts[i], flip) for i, flip in enumerate(FLIPS) if flip]
    low, high = after((tokens[:, :HALF], tokens[:, HALF:]), parts[0])
    right_0 = shift(low, "tensor", NZ, 1)
    left_0 = shift(high, "tensor", NZ, -1)
    fb_far = pltpu.with_memory_space_constraint(fb, pltpu.HBM)
    outgoing = pick(chosen, up, fb_far, [parts[0], *replies])
    vals = load(after(vals, outgoing))
    got_1 = dp_exchange(outgoing[None], lambda x, y, c: (x, y ^ 1, c), vals)
    high_n, low_n = after((high, low), outgoing)
    rest_0 = shift(high_n, "tensor", NZ, 1)
    rest_1 = shift(low_n, "tensor", NZ, -1)
    update = window(0, after(head, got_1), nxt, w1, w2, vals, None)
    got_2 = dp_exchange(got_1, lambda x, y, c: (x, y ^ 3, c), update)
    totals = first_products(up, after(fb, got_2), tokens, right_0, left_0)
    got_3 = dp_exchange(got_2, lambda x, y, c: (x ^ 1, y, c), totals)
    far_0 = shift(after(right_0, left_0), "tensor", NZ, 1)
    far_1 = shift(after(left_0, right_0), "tensor", NZ, -1)
    update = window(1, after(head, got_3), nxt, w1, w2, vals, update)
    got_4 = dp_exchange(got_3, lambda x, y, c: (x ^ 3, y, c), (update, rest_0, rest_1))
    totals = second_products(up, after(rest_0, got_4), rest_1, totals)
    got = dp_exchange(got_4, lambda x, y, c: (x, y, c ^ 1), totals)
    update_dir, newest_values = newest(head, nxt, w1, w2, got, vals, update)
    ready = after(chosen, newest_values)
    merged = end(ready, up, [far_0, far_1], totals)
    return (update_dir, merged[None], newest_values[None])


def solution(mesh):
    placed = (
        P("dp", "tensor", None),
        P("dp", None, "tensor"),
        P("dp", None, "tensor"),
        P("dp", "tensor", None),
        P(None, "tensor", None, None, None),
        P(None, "tensor", None),
        P(),
    )
    return jax.shard_map(
        local,
        mesh=mesh,
        in_specs=placed,
        out_specs=(P(None, "tensor"), P("dp", None, "tensor"), P("tensor", None, None, None)),
        check_vma=False,
    )
```
